32 devices in a mesh: slab: 8 (over z, y), rep: 4 (over x, core).
Axes of the slice: x: 2, y: 2, z: 4, core: 2. Of those that a mesh axis runs over, the one named last changes fastest.
Arguments:
- feats: bfloat16 [32768, 128], P(('slab', 'rep')), may hold values from -6 to 6
- cotangent: bfloat16 [32768, 128], P(('slab', 'rep')), may hold values from -6 to 6
- tile_table: bfloat16 [2048, 128, 128], P(('slab', 'rep')), as said below
- edge_src: int32 [32, 256], P(('slab', 'rep')), may hold values from 0 to 31
- edge_tile: int32 [32, 256], P(('slab', 'rep')), may hold values from 0 to 63
- edge_slot: int32 [32, 256], P(('slab', 'rep')), may hold values from 0 to 63
- edge_count: int32 [32], P(('slab', 'rep')), may hold values from 32 to 256, as said below
- slot_block: int32 [8, 64], replicated, may hold values from 0 to 31
- norm_gain: float32 [256], replicated, may hold values from 0.1 to 1.9
- w_in: bfloat16 [256, 512], replicated, may hold values from -0.375 to 0.375
- b_in: float32 [512], replicated, may hold values from -3 to 3
- w_out: bfloat16 [512, 128], replicated, may hold values from -0.25 to 0.25
Outputs:
- updated: bfloat16 [32768, 128], P(('slab', 'rep'))
- grad_feats: float32 [32768, 128], P(('slab', 'rep'))
- grad_gain: float32 [256], replicated
- grad_w_in: float32 [256, 512], replicated
- grad_b_in: float32 [512], replicated
- grad_w_out: float32 [512, 128], replicated
The draws below stay inside these ranges and needn't reach their ends.
Inputs may be any that keep to these rules, and one draw needn't show every extreme that they name: `edge_count`: some device uses all 256 entries and some only 32. `tile_table`: entries are zero or a positive edge weight.
All inputs are finite; a program needn't handle non-finite values.
Results may differ from the reference program's by a relative error of at most 0.0061.
Values may be sent and summed in bfloat16 or wider, within the bound.
A program may use at most 64 MiB of HBM per device.

```python
import jax
import jax.numpy as jnp
from jax import lax

W = 128
HID = 512
B = 128
NEIGH = 8
SLOT_CAP = 8
BLK_DEV = 8
EB = 256
TILE_DEV = 64
BLK_SLAB = 32
SLOTS = 64
DEV_COUNT = 32
NODES = 32768
TILES = 2048
N_SLAB = 8
N_REP = 4


def draw_tile_table(key, part):
    shape = (TILES, B, B)
    keep = jax.random.bernoulli(jax.random.fold_in(key, 1), min(0.5, 1.5 / B), shape)
    level = jax.random.uniform(jax.random.fold_in(key, 2), shape, jnp.float32)
    weights = 0.15 + 0.35 * level
    scaled = jnp.where(keep, weights, 0.0)
    return scaled.astype(jnp.float32).astype(jnp.bfloat16)


def draw_edge_count(key, part):
    least = EB // 8
    extent = EB - least
    rolled = jax.random.randint(jax.random.fold_in(key, 11), (DEV_COUNT,), 0, extent + 1)
    counts = least + rolled * rolled * rolled // max(extent * extent, 1)
    chosen = jax.random.randint(jax.random.fold_in(key, 12), (2,), 0, DEV_COUNT)
    busiest = chosen[0]
    lightest = (chosen[0] + 1 + chosen[1] % (DEV_COUNT - 1)) % DEV_COUNT
    device_ids = jnp.arange(DEV_COUNT)
    counts = jnp.where(device_ids == busiest, EB, counts)
    counts = jnp.where(device_ids == lightest, least, counts)
    return counts.astype(jnp.int32)


def touch_ends(drawn, own_key, low, largest):
    place = [jax.random.randint(jax.random.fold_in(own_key, axis), (), 0, length) for axis, length in enumerate(drawn.shape)]
    widest = drawn.shape.index(max(drawn.shape))
    beside = place[:widest] + [(place[widest] + 1) % drawn.shape[widest]] + place[widest + 1:]
    return drawn.at[tuple(place)].set(low).at[tuple(beside)].set(largest)


def block_levels(rng, shape, cuts, low, high):
    def one(axis_at, parts):
        steps = jax.random.uniform(jax.random.fold_in(jax.random.fold_in(rng, 6), axis_at), (parts,), jnp.float32, low / len(cuts), high / len(cuts))
        return jnp.repeat(jnp.exp(steps), shape[axis_at] // parts).reshape((-1,) + (1,) * (len(shape) - axis_at - 1))

    level = one(*cuts[0])
    for cut in cuts[1:]:
        level = level * one(*cut)
    return level


def gaussian(own_key, dims, width, most, cuts=(), held_as=jnp.bfloat16):
    array = width * jax.random.normal(own_key, dims, jnp.float32)
    if cuts:
        array = array * block_levels(own_key, dims, cuts, -0.22, 0.18)
    return jnp.clip(array, -most, most).astype(held_as)


def setup_inputs(seed: int = 0) -> dict:
    splits = jax.random.split(jax.random.key(seed), 13)
    feats = gaussian(splits[0], (NODES, W), 1.0, 6.0, ((0, 32),))
    cotangent = gaussian(splits[1], (NODES, W), 1.0, 6.0, ((0, 32),))
    tile_table = draw_tile_table(jax.random.fold_in(splits[12], 71), 0)
    edge_src = touch_ends(jax.random.randint(splits[3], (DEV_COUNT, EB), 0, BLK_SLAB), jax.random.fold_in(splits[3], 1), 0, BLK_SLAB - 1).astype(jnp.int32)
    edge_tile = touch_ends(jax.random.randint(splits[4], (DEV_COUNT, EB), 0, TILE_DEV), jax.random.fold_in(splits[4], 1), 0, TILE_DEV - 1).astype(jnp.int32)
    edge_slot = touch_ends(jax.random.randint(splits[5], (DEV_COUNT, EB), 0, SLOTS), jax.random.fold_in(splits[5], 1), 0, SLOTS - 1).astype(jnp.int32)
    edge_count = draw_edge_count(jax.random.fold_in(splits[12], 71), 0)
    slot_block = touch_ends(jax.random.randint(splits[7], (N_SLAB, SLOTS), 0, BLK_SLAB), jax.random.fold_in(splits[7], 1), 0, BLK_SLAB - 1).astype(jnp.int32)
    norm_gain = jnp.clip(1.0 + 0.18 * jax.random.normal(splits[8], (2 * W,), jnp.float32), 0.1, 1.9)
    w_in = gaussian(splits[9], (2 * W, HID), (2 * W) ** -0.5, 0.375)
    b_in = gaussian(splits[10], (HID,), 0.5, 3.0, (), jnp.float32)
    w_out = gaussian(splits[11], (HID, W), HID ** -0.5, 0.25)
    return {"feats": feats, "cotangent": cotangent, "tile_table": tile_table, "edge_src": edge_src, "edge_tile": edge_tile, "edge_slot": edge_slot, "edge_count": edge_count, "slot_block": slot_block, "norm_gain": norm_gain, "w_in": w_in, "b_in": b_in, "w_out": w_out}


RMS_EPS = 1e-06
EXACT_MODE = lax.Precision.HIGHEST

def node_forward(feat_rows, agg_rows, norm_gain, w_in, b_in, w_out):
    wide_in = jnp.concatenate([feat_rows.astype(jnp.float32), agg_rows], axis=1)
    inv_rms = lax.rsqrt(lax.optimization_barrier(jnp.mean(wide_in * wide_in, axis=1, keepdims=True)) + RMS_EPS)
    normed = (wide_in * inv_rms * norm_gain).astype(jnp.bfloat16)
    pre_act = jnp.dot(normed, w_in, preferred_element_type=jnp.float32) + b_in
    activated = jax.nn.silu(pre_act).astype(jnp.bfloat16)
    updated = (feat_rows.astype(jnp.float32) + jnp.dot(activated, w_out, preferred_element_type=jnp.float32)).astype(jnp.bfloat16)
    return (wide_in, inv_rms, normed, pre_act, activated, updated)

def node_backward(cot_rows, wide_in, inv_rms, normed, pre_act, activated, norm_gain, w_in, w_out):
    d_act = lax.dot_general(cot_rows, w_out, (((1,), (1,)), ((), ())), preferred_element_type=jnp.float32)
    sigmoid_pre = jax.nn.sigmoid(pre_act)
    d_pre = d_act * sigmoid_pre * (1.0 + pre_act * (1.0 - sigmoid_pre))
    d_pre_b = d_pre.astype(jnp.bfloat16)
    d_normed = lax.dot_general(d_pre_b, w_in, (((1,), (1,)), ((), ())), preferred_element_type=jnp.float32)
    d_scaled = d_normed * norm_gain
    inner_mean = lax.optimization_barrier(jnp.mean(d_scaled * wide_in, axis=1, keepdims=True))
    d_wide = inv_rms * d_scaled - inv_rms * inv_rms * inv_rms * wide_in * inner_mean
    grad_terms = (lax.optimization_barrier(jnp.sum(d_normed * wide_in * inv_rms, axis=0)), lax.dot_general(normed, d_pre_b, (((0,), (0,)), ((), ())), preferred_element_type=jnp.float32), lax.optimization_barrier(jnp.sum(d_pre, axis=0)), lax.dot_general(activated, cot_rows, (((0,), (0,)), ((), ())), preferred_element_type=jnp.float32))
    return (d_wide, grad_terms)

def reference(feats, cotangent, tile_table, edge_src, edge_tile, edge_slot, edge_count, slot_block, norm_gain, w_in, b_in, w_out):
    device_total = N_SLAB * N_REP
    block_total = N_SLAB * BLK_SLAB
    rows_dev = BLK_DEV * B
    slab_feats = feats.reshape(N_SLAB, BLK_SLAB, B, W)
    tile_sets = tile_table.reshape(device_total, TILE_DEV, B, B)
    slot_ids = jnp.arange(SLOTS, dtype=jnp.int32)
    slab_ids = jnp.arange(N_SLAB, dtype=jnp.int32)
    dest_slab = (slab_ids[:, None] + (slot_ids // SLOT_CAP)[None, :] - NEIGH // 2) % N_SLAB
    targets = (dest_slab * BLK_SLAB + slot_block).astype(jnp.int32)
    positions = jnp.arange(EB, dtype=jnp.int32)
    device_ids = jnp.arange(device_total, dtype=jnp.int32)

    def forward_device(aggregate, device):
        slab_no = device // N_REP
        is_live = positions < edge_count[device]
        sources = slab_feats[slab_no][edge_src[device]].astype(jnp.float32)
        tiles_now = tile_sets[device][edge_tile[device]].astype(jnp.float32)
        messages = jnp.einsum('eij,ejc->eic', tiles_now, sources, precision=EXACT_MODE)
        segment = jnp.where(is_live, edge_slot[device], SLOTS).astype(jnp.int32)
        partial_sums = jax.ops.segment_sum(messages, segment, num_segments=SLOTS + 1)[:SLOTS]
        return (aggregate.at[targets[slab_no]].add(partial_sums), None)
    aggregate = lax.scan(forward_device, jnp.zeros((block_total, B, W), jnp.float32), device_ids)[0]
    feat_dev = feats.reshape(device_total, rows_dev, W)
    cot_dev = cotangent.reshape(device_total, rows_dev, W)
    agg_dev = aggregate.reshape(device_total, rows_dev, W)

    def node_device(pieces):
        feat_rows, agg_rows, cot_rows = pieces
        wide_in, inv_rms, normed, pre_act, activated, updated = node_forward(feat_rows, agg_rows, norm_gain, w_in, b_in, w_out)
        d_wide, grad_terms = node_backward(cot_rows, wide_in, inv_rms, normed, pre_act, activated, norm_gain, w_in, w_out)
        return (updated, d_wide, grad_terms)
    updated, d_wide, grad_terms = lax.map(node_device, (feat_dev, agg_dev, cot_dev))
    scale = NODES ** (-0.5)
    grads = [lax.optimization_barrier(jnp.sum(term, axis=0)) * scale for term in grad_terms]
    d_agg = d_wide[:, :, W:].astype(jnp.bfloat16).reshape(block_total, B, W)

    def backward_device(from_edges, device):
        slab_no = device // N_REP
        is_live = positions < edge_count[device]
        slot_grads = d_agg[targets[slab_no]]
        grads_now = slot_grads[edge_slot[device]].astype(jnp.float32)
        tiles_now = tile_sets[device][edge_tile[device]].astype(jnp.float32)
        contrib = jnp.einsum('eji,ejc->eic', tiles_now, grads_now, precision=EXACT_MODE)
        segment = jnp.where(is_live, edge_src[device], BLK_SLAB).astype(jnp.int32)
        per_block = jax.ops.segment_sum(contrib, segment, num_segments=BLK_SLAB + 1)[:BLK_SLAB]
        return (from_edges.at[slab_no].add(per_block), None)
    from_edges = lax.scan(backward_device, jnp.zeros((N_SLAB, BLK_SLAB, B, W), jnp.float32), device_ids)[0]
    grad_feats = cotangent.astype(jnp.float32) + d_wide[:, :, :W].reshape(NODES, W) + from_edges.reshape(NODES, W)
    return (updated.reshape(NODES, W), grad_feats, grads[0], grads[1], grads[2], grads[3])
```

```python
import functools

import jax
import jax.numpy as jnp
from jax import lax
from jax.experimental import pallas as pl
from jax.experimental.pallas import tpu as pltpu
from jax.sharding import PartitionSpec as P

NEIGH = 8
SLOT_CAP = 8
MID = NEIGH // 2

RMS_EPS = 1e-06
EDGE_UNROLL = 8
AXES = ("slab", "rep")
VMEM = pl.BlockSpec(memory_space=pltpu.VMEM)
SMEM = pl.BlockSpec(memory_space=pltpu.SMEM)
DMA = pltpu.SemaphoreType.DMA


def remote(src, dst, send_sem, recv_sem, slab, rep):
    return pltpu.make_async_remote_copy(
        src_ref=src,
        dst_ref=dst,
        send_sem=send_sem,
        recv_sem=recv_sem,
        device_id=(slab, rep),
        device_id_type=pl.DeviceIdType.MESH,
    )


def greet(targets):
    barrier = pltpu.get_barrier_semaphore()
    for slab, rep in targets:
        pl.semaphore_signal(
            barrier, inc=1, device_id=(slab, rep), device_id_type=pl.DeviceIdType.MESH
        )
    pl.semaphore_wait(barrier, len(targets))


def place():
    slab, rep = lax.axis_index("slab"), lax.axis_index("rep")
    core = lax.rem(rep, 2)
    return slab, rep, core, lax.div(rep, 2), rep + 1 - 2 * core


def gather_rep(own, out, halves, pieces, send_sems, recv_sems, meanwhile):
    slab, rep, core, half, partner = place()
    rows = own.shape[0] // pieces

    def piece(ref, i):
        return ref.at[pl.ds(i * rows, rows)]

    far = []
    sems = 0
    for d in range(1, halves):
        peer = lax.rem(half + d, halves) * 2 + core
        for i in range(pieces):
            copy = remote(
                piece(own, i), piece(out.at[rep], i), send_sems.at[sems], recv_sems.at[sems], slab, peer
            )
            copy.start()
            far.append((copy, lax.rem(half + halves - d, halves) * 2 + core, i))
            sems += 1
    near = remote(own, out.at[rep], send_sems.at[sems], recv_sems.at[sems], slab, partner)
    near.start()
    sems += 1
    out[rep] = own[...]
    meanwhile()
    passed = [near]
    for copy, origin, i in far:
        copy.wait_recv()
        onward = remote(
            piece(out.at[origin], i),
            piece(out.at[origin], i),
            send_sems.at[sems],
            recv_sems.at[sems],
            slab,
            partner,
        )
        onward.start()
        passed.append(onward)
        sems += 1
    for copy in passed:
        copy.wait_recv()
    return [copy for copy, _, _ in far] + passed


def gather_sems(halves, pieces):
    return 2 * (halves - 1) * pieces + 1


def rep_targets(halves):
    slab, rep, core, half, partner = place()
    return [(slab, partner)] + [
        (slab, lax.rem(half + d, halves) * 2 + core) for d in range(1, halves)
    ]


def gather_kernel(halves, pieces, own, table_hbm, out, turned, table, table_sem, send_sems, recv_sems):
    load = pltpu.make_async_copy(table_hbm, table, table_sem)
    load.start()
    greet(rep_targets(halves))

    def meanwhile():
        load.wait()

        @pl.loop(0, table.shape[0])
        def _(t):
            turned[t] = table[t].T

    for copy in gather_rep(own, out, halves, pieces, send_sems, recv_sems, meanwhile):
        copy.wait_send()


def edge_kernel(by_slot, n_out, count, srcs, tiles, slots, table, given, out, acc):
    live = count[0]
    last = srcs.shape[1] - 1
    acc[...] = jnp.zeros_like(acc)

    def turn(i, carry):
        work = []
        for u in range(EDGE_UNROLL):
            at = i * EDGE_UNROLL + u
            e = jnp.minimum(at, last)
            src, slot = srcs[0, e], slots[0, e]
            read, write = (slot, src) if by_slot else (src, slot)
            product = jnp.dot(table[tiles[0, e]], given[read], preferred_element_type=jnp.float32)
            work.append((jnp.where(at < live, write, n_out), product))
        for write, product in work:
            acc[write] += product
        return carry

    lax.fori_loop(0, lax.div(live + EDGE_UNROLL - 1, EDGE_UNROLL), turn, 0)
    out[...] = acc[0:n_out].astype(out.dtype)


def edges(by_slot, n_out, count, srcs, tiles, slots, table, given):
    shape = (table.shape[1], given.shape[2])
    return pl.pallas_call(
        functools.partial(edge_kernel, by_slot, n_out),
        out_shape=jax.ShapeDtypeStruct((n_out, *shape), jnp.bfloat16),
        in_specs=[SMEM] * 4 + [VMEM] * 2,
        out_specs=VMEM,
        scratch_shapes=[pltpu.VMEM((n_out + 1, *shape), jnp.float32)],
    )(count, srcs, tiles, slots, table, given)


def slab_at(offset):
    n_slab = lax.axis_size("slab")
    return lax.rem(lax.axis_index("slab") + offset + n_slab, n_slab)


FAR_FIRST = sorted((g for g in range(NEIGH) if g != MID), key=lambda g: -abs(g - MID))
ORDER = FAR_FIRST + [MID]


def share(arrived, second, far_s, far_r, on_s, on_r, halves, meanwhile):
    slab, rep, core, half, partner = place()
    order = [MID] + FAR_FIRST[::-1]
    copies = []
    across = []
    for g in order:
        if g in second:
            second[g].wait_recv()
        own = arrived.at[g, core, half]
        for d in range(1, halves):
            peer = lax.rem(half + d, halves) * 2 + core
            copy = remote(own, own, far_s.at[d - 1, g], far_r.at[d - 1, g], slab, peer)
            copy.start()
            across.append((g, d, copy))
        copy = remote(own, own, on_s.at[0, g], on_r.at[0, g], slab, partner)
        copy.start()
        copies.append(copy)
    meanwhile()
    for g, d, copy in across:
        copy.wait_recv()
        theirs = arrived.at[g, core, lax.rem(half + halves - d, halves)]
        onward = remote(theirs, theirs, on_s.at[d, g], on_r.at[d, g], slab, partner)
        onward.start()
        copies.append(onward)
    for copy in copies:
        copy.wait_recv()
    for copy in copies + [copy for _, _, copy in across] + list(second.values()):
        copy.wait_send()


def spread_kernel(
    halves,
    part,
    arrived,
    from_core,
    to_far,
    from_far,
    outgoing,
    core_s,
    core_r,
    fold_s,
    fold_r,
    slab_s,
    slab_r,
    far_s,
    far_r,
    on_s,
    on_r,
):
    slab, rep, core, half, partner = place()
    greet(rep_targets(halves) + [(slab_at(MID - g), rep) for g in FAR_FIRST])
    f32 = jnp.float32
    first = {}
    for g in ORDER:
        first[g] = remote(
            part.at[g, 1 - core], from_core.at[g], core_s.at[g], core_r.at[g], slab, partner
        )
        first[g].start()
    cross = {}
    for g in ORDER:
        first[g].wait_recv()
        for d in range(1, halves):
            h = lax.rem(half + d, halves)
            total = part[g, core, h].astype(f32) + from_core[g, h].astype(f32)
            to_far[d - 1, g] = total.astype(jnp.bfloat16)
            cross[g, d] = remote(
                to_far.at[d - 1, g],
                from_far.at[d - 1, g],
                fold_s.at[d - 1, g],
                fold_r.at[d - 1, g],
                slab,
                h * 2 + core,
            )
            cross[g, d].start()
    second = {}
    for g in ORDER:
        total = part[g, core, half].astype(f32) + from_core[g, half].astype(f32)
        for d in range(1, halves):
            cross[g, d].wait_recv()
            total = total + from_far[d - 1, g].astype(f32)
        if g == MID:
            arrived[g, core, half] = total.astype(jnp.bfloat16)
        else:
            outgoing[g] = total.astype(jnp.bfloat16)
            second[g] = remote(
                outgoing.at[g],
                arrived.at[g, core, half],
                slab_s.at[g],
                slab_r.at[g],
                slab_at(g - MID),
                rep,
            )
            second[g].start()
    share(arrived, second, far_s, far_r, on_s, on_r, halves, lambda: None)
    for copy in list(first.values()) + list(cross.values()):
        copy.wait_send()


def node_kernel(
    slot_block,
    arrived,
    feats,
    cot,
    gain,
    w_in,
    b_in,
    w_out,
    updated,
    base,
    d_agg,
    packed,
    agg,
    g_in,
    g_out,
    g_gain,
    g_b,
):
    slab, rep = lax.axis_index("slab"), lax.axis_index("rep")
    f32, bf16 = jnp.float32, jnp.bfloat16
    own_blocks, block_rows, width = agg.shape
    n_slab = slot_block.shape[0]
    agg[...] = jnp.zeros_like(agg)

    @pl.loop(0, NEIGH * SLOT_CAP)
    def _(c):
        origin = lax.rem(slab - (lax.div(c, SLOT_CAP) - MID) + n_slab, n_slab)
        dest = slot_block[origin, c]

        @pl.when(lax.div(dest, own_blocks) == rep)
        def _():
            agg[lax.rem(dest, own_blocks)] += arrived[c].astype(f32)

    for ref in (g_in, g_out, g_gain, g_b):
        ref[...] = jnp.zeros_like(ref)
    step_blocks = 2 if own_blocks % 2 == 0 else 1
    rows = step_blocks * block_rows

    @pl.loop(0, own_blocks // step_blocks)
    def _(i):
        at = pl.ds(pl.multiple_of(i * rows, rows), rows)
        feat = feats[at].astype(f32)
        cots = cot[at]
        wide = jnp.concatenate(
            [feat, agg[pl.ds(i * step_blocks, step_blocks)].reshape(rows, width)], axis=1
        )
        inv = lax.rsqrt(jnp.mean(wide * wide, axis=1, keepdims=True) + RMS_EPS)
        scaled = wide * inv
        normed = (scaled * gain[...]).astype(bf16)
        pre = jnp.dot(normed, w_in[...], preferred_element_type=f32) + b_in[...]
        sg = jax.nn.sigmoid(pre)
        act = (pre * sg).astype(bf16)
        updated[at] = (feat + jnp.dot(act, w_out[...], preferred_element_type=f32)).astype(bf16)
        d_act = lax.dot_general(cots, w_out[...], (((1,), (1,)), ((), ())), preferred_element_type=f32)
        d_pre = d_act * sg * (1.0 + pre * (1.0 - sg))
        d_pre_b = d_pre.astype(bf16)
        d_normed = lax.dot_general(
            d_pre_b, w_in[...], (((1,), (1,)), ((), ())), preferred_element_type=f32
        )
        d_scaled = d_normed * gain[...]
        inner = jnp.mean(d_scaled * wide, axis=1, keepdims=True)
        d_wide = inv * d_scaled - inv * inv * inv * wide * inner
        base[at] = cots.astype(f32) + d_wide[:, :width]
        d_agg[at] = d_wide[:, width:].astype(bf16)
        g_in[...] += lax.dot_general(normed, d_pre_b, (((0,), (0,)), ((), ())), preferred_element_type=f32)
        g_out[...] += lax.dot_general(act, cots, (((0,), (0,)), ((), ())), preferred_element_type=f32)
        g_gain[...] += jnp.sum(d_normed * scaled, axis=0, keepdims=True)
        g_b[...] += jnp.sum(d_pre, axis=0, keepdims=True)

    packed[...] = jnp.zeros_like(packed)
    n = g_in.shape[0]
    for c in range(g_in.shape[1] // width):
        packed[n * c : n * (c + 1)] = g_in[:, width * c : width * (c + 1)].astype(bf16)
    n = n * (g_in.shape[1] // width)
    packed[n : n + g_out.shape[0]] = g_out[...].astype(bf16)
    n += g_out.shape[0]
    rest = [
        ref[:, width * c : width * (c + 1)]
        for ref in (g_gain, g_b)
        for c in range(ref.shape[1] // width)
    ]
    rest.append(jnp.zeros((16 - len(rest), width), f32))
    packed[n : n + 16] = jnp.concatenate(rest, axis=0).astype(bf16)


def return_kernel(
    halves,
    pieces,
    slot_block,
    own,
    grads,
    arrived,
    summed,
    gathered,
    outgoing,
    w_core,
    w_to,
    w_far,
    w_rep,
    w_in,
    w_piece,
    gat_s,
    gat_r,
    slab_s,
    slab_r,
    far_s,
    far_r,
    on_s,
    on_r,
    wc_s,
    wc_r,
    wf_s,
    wf_r,
    ws_s,
    ws_r,
    wg_s,
    wg_r,
):
    slab, rep, core, half, partner = place()
    n_slab = slot_block.shape[0]
    peers = range(1, n_slab)
    greet(rep_targets(halves) + [(slab_at(d), rep) for d in peers])
    f32, bf16 = jnp.float32, jnp.bfloat16
    own_blocks = own.shape[0]
    per_rep = outgoing.shape[1]
    sent = []
    w_cross = []

    def halves_of_weights():
        near = []
        for d in list(range(1, halves)) + [0]:
            h = lax.rem(half + d, halves)
            copy = remote(grads.at[h, 1 - core], w_core.at[h], wc_s.at[d], wc_r.at[d], slab, partner)
            copy.start()
            near.append((d, h, copy))
        for d, h, copy in near:
            copy.wait_recv()
            if d > 0:
                total = grads[h, core].astype(f32) + w_core[h].astype(f32)
                w_to[d - 1] = total.astype(bf16)
                cross = remote(
                    w_to.at[d - 1], w_far.at[d - 1], wf_s.at[d - 1], wf_r.at[d - 1], slab, h * 2 + core
                )
                cross.start()
                w_cross.append(cross)
            sent.append(copy)

    sent += gather_rep(own, gathered, halves, pieces, gat_s, gat_r, halves_of_weights)
    second = {}
    for g in ORDER:
        origin = slab_at(MID - g)
        for j in range(per_rep):
            dest = slot_block[origin, g * SLOT_CAP + (half + core * halves) * per_rep + j]
            picked = gathered[lax.div(dest, own_blocks), lax.rem(dest, own_blocks)]
            if g == MID:
                arrived[g, core, half, j] = picked
            else:
                outgoing[g, j] = picked
        if g != MID:
            second[g] = remote(
                outgoing.at[g], arrived.at[g, core, half], slab_s.at[g], slab_r.at[g], origin, rep
            )
            second[g].start()
    total = grads[half, core].astype(f32) + w_core[half].astype(f32)
    for d, copy in enumerate(w_cross):
        copy.wait_recv()
        total = total + w_far[d].astype(f32)
    w_rep[...] = total.astype(bf16)
    w_slab = []
    for d in peers:
        peer = slab_at(d)
        copy = remote(w_rep.at[peer], w_in.at[d - 1], ws_s.at[d - 1], ws_r.at[d - 1], peer, rep)
        copy.start()
        w_slab.append(copy)
    w_back = []

    def finish_weights():
        total = w_rep[slab].astype(f32)
        for d, copy in enumerate(w_slab):
            copy.wait_recv()
            total = total + w_in[d].astype(f32)
        w_piece[...] = total.astype(bf16)
        summed[slab] = total.astype(bf16)
        for d in peers:
            copy = remote(
                w_piece, summed.at[slab], wg_s.at[d - 1], wg_r.at[d - 1], slab_at(d), rep
            )
            copy.start()
            w_back.append(copy)

    share(arrived, second, far_s, far_r, on_s, on_r, halves, finish_weights)
    for copy in w_back:
        copy.wait_recv()
    for copy in sent + w_cross + w_slab + w_back:
        copy.wait_send()


def fold_kernel(
    halves, part, summed, out, grads, from_core, outgoing, from_far, core_s, core_r, far_s, far_r, gat_s, gat_r
):
    slab, rep, core, half, partner = place()
    f32 = jnp.float32
    greet(rep_targets(halves))
    near = []
    for d in list(range(1, halves)) + [0]:
        h = lax.rem(half + d, halves)
        copy = remote(part.at[h, 1 - core], from_core.at[h], core_s.at[d], core_r.at[d], slab, partner)
        copy.start()
        near.append((d, h, copy))
    far = []

    def fold():
        for d, h, copy in near:
            copy.wait_recv()
            total = part[h, core].astype(f32) + from_core[h].astype(f32)
            if d == 0:
                out[...] = total
            else:
                outgoing[d - 1] = total.astype(jnp.bfloat16)
                onward = remote(
                    outgoing.at[d - 1],
                    from_far.at[d - 1],
                    far_s.at[d - 1],
                    far_r.at[d - 1],
                    slab,
                    h * 2 + core,
                )
                onward.start()
                far.append(onward)

    sent = gather_rep(summed, grads, halves, 1, gat_s, gat_r, fold)
    for d, onward in enumerate(far):
        onward.wait_recv()
        out[...] += from_far[d].astype(f32)
    for copy in sent + far + [copy for _, _, copy in near]:
        copy.wait_send()


def comm(kernel, cid, out_shape, in_specs, scratch):
    return pl.pallas_call(
        kernel,
        out_shape=out_shape,
        in_specs=in_specs,
        out_specs=jax.tree.map(lambda _: VMEM, out_shape),
        scratch_shapes=scratch,
        compiler_params=pltpu.CompilerParams(collective_id=cid, has_side_effects=True),
    )


def body(
    feats,
    cotangent,
    tile_table,
    edge_src,
    edge_tile,
    edge_slot,
    edge_count,
    slot_block,
    norm_gain,
    w_in,
    b_in,
    w_out,
):
    n_slab = lax.axis_size("slab")
    n_rep = lax.axis_size("rep")
    halves = n_rep // 2
    rows_dev, width = feats.shape
    hidden = w_out.shape[0]
    block_rows = tile_table.shape[1]
    own_blocks = rows_dev // block_rows
    slab_blocks = own_blocks * n_rep
    slot_count = slot_block.shape[1]
    per_rep = SLOT_CAP // n_rep
    pieces = 4
    bf16, f32 = jnp.bfloat16, jnp.float32
    lists = (edge_count, edge_src, edge_tile, edge_slot)
    shape = jax.ShapeDtypeStruct

    def block(*lead):
        return pltpu.VMEM((*lead, block_rows, width), bf16)

    n_gat = gather_sems(halves, pieces)
    slab_feats, turned = comm(
        functools.partial(gather_kernel, halves, pieces),
        0,
        (
            shape((n_rep, own_blocks, block_rows, width), bf16),
            shape(tile_table.shape, bf16),
        ),
        [VMEM, pl.BlockSpec(memory_space=pl.ANY)],
        [pltpu.VMEM(tile_table.shape, bf16), DMA] + [DMA((n_gat,))] * 2,
    )(feats.reshape(own_blocks, block_rows, width), tile_table)
    slab_feats = slab_feats.reshape(slab_blocks, block_rows, width)
    partial_sums = edges(False, slot_count, *lists, tile_table, slab_feats)
    arrived_shape = (NEIGH, 2, halves, per_rep, block_rows, width)
    share_sems = [DMA((halves - 1, NEIGH))] * 2 + [DMA((halves, NEIGH))] * 2
    arrived = comm(
        functools.partial(spread_kernel, halves),
        1,
        shape(arrived_shape, bf16),
        [VMEM],
        [
            block(NEIGH, halves, per_rep),
            block(halves - 1, NEIGH, per_rep),
            block(halves - 1, NEIGH, per_rep),
            block(NEIGH, per_rep),
        ]
        + [DMA((NEIGH,))] * 2
        + [DMA((halves - 1, NEIGH))] * 2
        + [DMA((NEIGH,))] * 2
        + share_sems,
    )(partial_sums.reshape(arrived_shape))
    used = w_in.size // width + hidden + 16
    each = -(-used // (n_slab * n_rep * 16)) * 16
    updated, base, d_agg, packed = pl.pallas_call(
        node_kernel,
        out_shape=(
            shape((rows_dev, width), bf16),
            shape((rows_dev, width), f32),
            shape((rows_dev, width), bf16),
            shape((n_slab * n_rep * each, width), bf16),
        ),
        in_specs=[SMEM] + [VMEM] * 7,
        out_specs=(VMEM,) * 4,
        scratch_shapes=[
            pltpu.VMEM((own_blocks, block_rows, width), f32),
            pltpu.VMEM(w_in.shape, f32),
            pltpu.VMEM(w_out.shape, f32),
            pltpu.VMEM((1, 2 * width), f32),
            pltpu.VMEM((1, hidden), f32),
        ],
    )(
        slot_block,
        arrived.reshape(slot_count, block_rows, width),
        feats,
        cotangent,
        norm_gain.reshape(1, -1),
        w_in,
        b_in.reshape(1, -1),
        w_out,
    )
    weights = pltpu.VMEM((n_slab, each, width), bf16)
    many = pltpu.VMEM((halves - 1, n_slab, each, width), bf16)
    slot_grads, summed = comm(
        functools.partial(return_kernel, halves, pieces),
        2,
        (shape(arrived_shape, bf16), shape((n_slab, each, width), bf16)),
        [SMEM, VMEM, VMEM],
        [
            block(n_rep, own_blocks),
            block(NEIGH, per_rep),
            pltpu.VMEM((halves, n_slab, each, width), bf16),
            many,
            many,
            weights,
            pltpu.VMEM((n_slab - 1, each, width), bf16),
            pltpu.VMEM((each, width), bf16),
        ]
        + [DMA((n_gat,))] * 2
        + [DMA((NEIGH,))] * 2
        + share_sems
        + [DMA((halves,))] * 2
        + [DMA((halves - 1,))] * 2
        + [DMA((n_slab - 1,))] * 4,
    )(
        slot_block,
        d_agg.reshape(own_blocks, block_rows, width),
        packed.reshape(halves, 2, n_slab, each, width),
    )
    from_edges = edges(
        True, slab_blocks, *lists, turned, slot_grads.reshape(slot_count, block_rows, width)
    )
    n_sum = gather_sems(halves, 1)
    folded, grads = comm(
        functools.partial(fold_kernel, halves),
        3,
        (shape((rows_dev, width), f32), shape((n_rep, n_slab, each, width), bf16)),
        [VMEM, VMEM],
        [
            pltpu.VMEM((halves, rows_dev, width), bf16),
            pltpu.VMEM((halves - 1, rows_dev, width), bf16),
            pltpu.VMEM((halves - 1, rows_dev, width), bf16),
        ]
        + [DMA((halves,))] * 2
        + [DMA((halves - 1,))] * 2
        + [DMA((n_sum,))] * 2,
    )(from_edges.reshape(halves, 2, rows_dev, width), summed)
    grad_feats = base + folded
    scale = float(rows_dev * n_slab * n_rep) ** (-0.5)
    grads = grads.reshape(-1, width)
    panels = hidden // width
    n = 2 * width * panels
    grad_w_in = grads[:n].reshape(panels, 2 * width, width).swapaxes(0, 1).reshape(2 * width, hidden)
    grad_w_out = grads[n : n + hidden]
    n += hidden
    grad_gain = grads[n : n + 2].reshape(-1)
    grad_b_in = grads[n + 2 : n + 2 + panels].reshape(-1)
    return (
        updated,
        grad_feats,
        grad_gain.astype(f32) * scale,
        grad_w_in.astype(f32) * scale,
        grad_b_in.astype(f32) * scale,
        grad_w_out.astype(f32) * scale,
    )


def solution(mesh):
    placed = (
        P(("slab", "rep"), None),
        P(("slab", "rep"), None),
        P(("slab", "rep"), None, None),
        P(("slab", "rep"), None),
        P(("slab", "rep"), None),
        P(("slab", "rep"), None),
        P(("slab", "rep")),
        P(),
        P(),
        P(),
        P(),
        P(),
    )
    return jax.shard_map(
        body,
        mesh=mesh,
        in_specs=placed,
        out_specs=(P(("slab", "rep"), None), P(("slab", "rep"), None), P(), P(), P(), P()),
        check_vma=False,
    )
```

```python
import functools

import jax
import jax.numpy as jnp
from jax import lax
from jax.experimental import pallas as pl
from jax.experimental.pallas import tpu as pltpu
from jax.sharding import PartitionSpec as P

NEIGH = 8
SLOT_CAP = 8
MID = NEIGH // 2

RMS_EPS = 1e-06
EDGE_UNROLL = 8
AXES = ("slab", "rep")
VMEM = pl.BlockSpec(memory_space=pltpu.VMEM)
SMEM = pl.BlockSpec(memory_space=pltpu.SMEM)
DMA = pltpu.SemaphoreType.DMA


def remote(src, dst, send_sem, recv_sem, slab, rep):
    return pltpu.make_async_remote_copy(
        src_ref=src,
        dst_ref=dst,
        send_sem=send_sem,
        recv_sem=recv_sem,
        device_id=(slab, rep),
        device_id_type=pl.DeviceIdType.MESH,
    )


def greet(targets):
    barrier = pltpu.get_barrier_semaphore()
    for slab, rep in targets:
        pl.semaphore_signal(
            barrier, inc=1, device_id=(slab, rep), device_id_type=pl.DeviceIdType.MESH
        )
    pl.semaphore_wait(barrier, len(targets))


def place():
    slab, rep = lax.axis_index("slab"), lax.axis_index("rep")
    core = lax.rem(rep, 2)
    return slab, rep, core, lax.div(rep, 2), rep + 1 - 2 * core


def gather_rep(own, out, halves, pieces, send_sems, recv_sems, meanwhile):
    slab, rep, core, half, partner = place()
    rows = own.shape[0] // pieces

    def piece(ref, i):
        return ref.at[pl.ds(i * rows, rows)]

    far = []
    sems = 0
    for d in range(1, halves):
        peer = lax.rem(half + d, halves) * 2 + core
        for i in range(pieces):
            copy = remote(
                piece(own, i), piece(out.at[rep], i), send_sems.at[sems], recv_sems.at[sems], slab, peer
            )
            copy.start()
            far.append((copy, lax.rem(half + halves - d, halves) * 2 + core, i))
            sems += 1
    near = remote(own, out.at[rep], send_sems.at[sems], recv_sems.at[sems], slab, partner)
    near.start()
    sems += 1
    out[rep] = own[...]
    meanwhile()
    passed = [near]
    for copy, origin, i in far:
        copy.wait_recv()
        onward = remote(
            piece(out.at[origin], i),
            piece(out.at[origin], i),
            send_sems.at[sems],
            recv_sems.at[sems],
            slab,
            partner,
        )
        onward.start()
        passed.append(onward)
        sems += 1
    for copy in passed:
        copy.wait_recv()
    return [copy for copy, _, _ in far] + passed


def gather_sems(halves, pieces):
    return 2 * (halves - 1) * pieces + 1


def rep_targets(halves):
    slab, rep, core, half, partner = place()
    return [(slab, partner)] + [
        (slab, lax.rem(half + d, halves) * 2 + core) for d in range(1, halves)
    ]


def gather_kernel(halves, pieces, own, table_hbm, out, turned, table, table_sem, send_sems, recv_sems):
    load = pltpu.make_async_copy(table_hbm, table, table_sem)
    load.start()
    greet(rep_targets(halves))

    def meanwhile():
        load.wait()

        @pl.loop(0, table.shape[0])
        def _(t):
            turned[t] = table[t].T

    for copy in gather_rep(own, out, halves, pieces, send_sems, recv_sems, meanwhile):
        copy.wait_send()


def edge_kernel(by_slot, n_out, count, srcs, tiles, slots, table, given, out, acc):
    live = count[0]
    last = srcs.shape[1] - 1
    acc[...] = jnp.zeros_like(acc)

    def turn(i, carry):
        work = []
        for u in range(EDGE_UNROLL):
            at = i * EDGE_UNROLL + u
            e = jnp.minimum(at, last)
            src, slot = srcs[0, e], slots[0, e]
            read, write = (slot, src) if by_slot else (src, slot)
            product = jnp.dot(table[tiles[0, e]], given[read], preferred_element_type=jnp.float32)
            work.append((jnp.where(at < live, write, n_out), product))
        for write, product in work:
            acc[write] += product
        return carry

    lax.fori_loop(0, lax.div(live + EDGE_UNROLL - 1, EDGE_UNROLL), turn, 0)
    out[...] = acc[0:n_out].astype(out.dtype)


def edges(by_slot, n_out, count, srcs, tiles, slots, table, given):
    shape = (table.shape[1], given.shape[2])
    return pl.pallas_call(
        functools.partial(edge_kernel, by_slot, n_out),
        out_shape=jax.ShapeDtypeStruct((n_out, *shape), jnp.bfloat16),
        in_specs=[SMEM] * 4 + [VMEM] * 2,
        out_specs=VMEM,
        scratch_shapes=[pltpu.VMEM((n_out + 1, *shape), jnp.float32)],
    )(count, srcs, tiles, slots, table, given)


def slab_at(offset):
    n_slab = lax.axis_size("slab")
    return lax.rem(lax.axis_index("slab") + offset + n_slab, n_slab)


FAR_FIRST = sorted((g for g in range(NEIGH) if g != MID), key=lambda g: -abs(g - MID))
ORDER = FAR_FIRST + [MID]


def share(arrived, second, direct, crossing, far_s, far_r, on_s, on_r, straight_s, straight_r, halves, meanwhile):
    slab, rep, core, half, partner = place()
    order = [MID] + FAR_FIRST
    copies = []
    across = []
    for g in order:
        if g in second:
            second[g].wait_recv()
        own = arrived.at[g, core, half, pl.ds(0, crossing)]
        for d in range(1, halves):
            peer = lax.rem(half + d, halves) * 2 + core
            copy = remote(own, own, far_s.at[d - 1, g], far_r.at[d - 1, g], slab, peer)
            copy.start()
            across.append((g, d, copy))
        copy = remote(own, own, on_s.at[0, g], on_r.at[0, g], slab, partner)
        copy.start()
        copies.append(copy)
    meanwhile()
    for g, d, copy in across:
        copy.wait_recv()
        theirs = arrived.at[g, core, lax.rem(half + halves - d, halves), pl.ds(0, crossing)]
        onward = remote(theirs, theirs, on_s.at[d, g], on_r.at[d, g], slab, partner)
        onward.start()
        copies.append(onward)
    others = arrived.shape[3] - crossing
    if others:
        for g in order:
            for h in range(halves):
                if (g, h) in direct:
                    direct[g, h].wait_recv()
                here = arrived.at[g, core, h, pl.ds(crossing, others)]
                onward = remote(here, here, straight_s.at[h, g], straight_r.at[h, g], slab, partner)
                onward.start()
                copies.append(onward)
    for copy in copies:
        copy.wait_recv()
    sent = copies + [copy for _, _, copy in across] + list(second.values()) + list(direct.values())
    for copy in sent:
        copy.wait_send()


def spread_kernel(
    halves,
    part,
    arrived,
    from_core,
    to_far,
    from_far,
    outgoing,
    core_s,
    core_r,
    fold_s,
    fold_r,
    slab_s,
    slab_r,
    far_s,
    far_r,
    on_s,
    on_r,
):
    slab, rep, core, half, partner = place()
    greet(rep_targets(halves) + [(slab_at(MID - g), rep) for g in FAR_FIRST])
    f32 = jnp.float32
    first = {}
    for g in ORDER:
        first[g] = remote(
            part.at[g, 1 - core], from_core.at[g], core_s.at[g], core_r.at[g], slab, partner
        )
        first[g].start()
    cross = {}
    for g in ORDER:
        first[g].wait_recv()
        for d in range(1, halves):
            h = lax.rem(half + d, halves)
            total = part[g, core, h].astype(f32) + from_core[g, h].astype(f32)
            to_far[d - 1, g] = total.astype(jnp.bfloat16)
            cross[g, d] = remote(
                to_far.at[d - 1, g],
                from_far.at[d - 1, g],
                fold_s.at[d - 1, g],
                fold_r.at[d - 1, g],
                slab,
                h * 2 + core,
            )
            cross[g, d].start()
    second = {}
    for g in ORDER:
        total = part[g, core, half].astype(f32) + from_core[g, half].astype(f32)
        for d in range(1, halves):
            cross[g, d].wait_recv()
            total = total + from_far[d - 1, g].astype(f32)
        if g == MID:
            arrived[g, core, half] = total.astype(jnp.bfloat16)
        else:
            outgoing[g] = total.astype(jnp.bfloat16)
            second[g] = remote(
                outgoing.at[g],
                arrived.at[g, core, half],
                slab_s.at[g],
                slab_r.at[g],
                slab_at(g - MID),
                rep,
            )
            second[g].start()
    share(
        arrived,
        second,
        {},
        arrived.shape[3],
        far_s,
        far_r,
        on_s,
        on_r,
        None,
        None,
        halves,
        lambda: None,
    )
    for copy in list(first.values()) + list(cross.values()):
        copy.wait_send()


def node_kernel(
    slot_block,
    arrived,
    feats,
    cot,
    gain,
    w_in,
    b_in,
    w_out,
    updated,
    base,
    d_agg,
    packed,
    agg,
    g_in,
    g_out,
    g_gain,
    g_b,
):
    slab, rep = lax.axis_index("slab"), lax.axis_index("rep")
    f32, bf16 = jnp.float32, jnp.bfloat16
    own_blocks, block_rows, width = agg.shape
    n_slab = slot_block.shape[0]
    agg[...] = jnp.zeros_like(agg)

    @pl.loop(0, NEIGH * SLOT_CAP)
    def _(c):
        origin = lax.rem(slab - (lax.div(c, SLOT_CAP) - MID) + n_slab, n_slab)
        dest = slot_block[origin, c]

        @pl.when(lax.div(dest, own_blocks) == rep)
        def _():
            agg[lax.rem(dest, own_blocks)] += arrived[c].astype(f32)

    for ref in (g_in, g_out, g_gain, g_b):
        ref[...] = jnp.zeros_like(ref)
    step_blocks = 2 if own_blocks % 2 == 0 else 1
    rows = step_blocks * block_rows

    @pl.loop(0, own_blocks // step_blocks)
    def _(i):
        at = pl.ds(pl.multiple_of(i * rows, rows), rows)
        feat = feats[at].astype(f32)
        cots = cot[at]
        wide = jnp.concatenate(
            [feat, agg[pl.ds(i * step_blocks, step_blocks)].reshape(rows, width)], axis=1
        )
        inv = lax.rsqrt(jnp.mean(wide * wide, axis=1, keepdims=True) + RMS_EPS)
        scaled = wide * inv
        normed = (scaled * gain[...]).astype(bf16)
        pre = jnp.dot(normed, w_in[...], preferred_element_type=f32) + b_in[...]
        sg = jax.nn.sigmoid(pre)
        act = (pre * sg).astype(bf16)
        updated[at] = (feat + jnp.dot(act, w_out[...], preferred_element_type=f32)).astype(bf16)
        d_act = lax.dot_general(cots, w_out[...], (((1,), (1,)), ((), ())), preferred_element_type=f32)
        d_pre = d_act * sg * (1.0 + pre * (1.0 - sg))
        d_pre_b = d_pre.astype(bf16)
        d_normed = lax.dot_general(
            d_pre_b, w_in[...], (((1,), (1,)), ((), ())), preferred_element_type=f32
        )
        d_scaled = d_normed * gain[...]
        inner = jnp.mean(d_scaled * wide, axis=1, keepdims=True)
        d_wide = inv * d_scaled - inv * inv * inv * wide * inner
        base[at] = cots.astype(f32) + d_wide[:, :width]
        d_agg[at] = d_wide[:, width:].astype(bf16)
        g_in[...] += lax.dot_general(normed, d_pre_b, (((0,), (0,)), ((), ())), preferred_element_type=f32)
        g_out[...] += lax.dot_general(act, cots, (((0,), (0,)), ((), ())), preferred_element_type=f32)
        g_gain[...] += jnp.sum(d_normed * scaled, axis=0, keepdims=True)
        g_b[...] += jnp.sum(d_pre, axis=0, keepdims=True)

    packed[...] = jnp.zeros_like(packed)
    n = g_in.shape[0]
    for c in range(g_in.shape[1] // width):
        packed[n * c : n * (c + 1)] = g_in[:, width * c : width * (c + 1)].astype(bf16)
    n = n * (g_in.shape[1] // width)
    packed[n : n + g_out.shape[0]] = g_out[...].astype(bf16)
    n += g_out.shape[0]
    rest = [
        ref[:, width * c : width * (c + 1)]
        for ref in (g_gain, g_b)
        for c in range(ref.shape[1] // width)
    ]
    rest.append(jnp.zeros((16 - len(rest), width), f32))
    packed[n : n + 16] = jnp.concatenate(rest, axis=0).astype(bf16)


def return_kernel(
    halves,
    pieces,
    slot_block,
    own,
    grads,
    arrived,
    summed,
    gathered,
    outgoing,
    plain,
    w_core,
    w_to,
    w_far,
    w_rep,
    w_in,
    w_piece,
    gat_s,
    gat_r,
    slab_s,
    slab_r,
    far_s,
    far_r,
    on_s,
    on_r,
    plain_s,
    plain_r,
    straight_s,
    straight_r,
    wc_s,
    wc_r,
    wf_s,
    wf_r,
    ws_s,
    ws_r,
    wg_s,
    wg_r,
):
    slab, rep, core, half, partner = place()
    n_slab = slot_block.shape[0]
    peers = range(1, n_slab)
    greet(rep_targets(halves) + [(slab_at(d), rep) for d in peers])
    f32, bf16 = jnp.float32, jnp.bfloat16
    own_blocks = own.shape[0]
    per_rep = arrived.shape[3]
    crossing = outgoing.shape[1]
    sent = []
    w_cross = []

    def halves_of_weights():
        near = []
        for d in list(range(1, halves)) + [0]:
            h = lax.rem(half + d, halves)
            copy = remote(grads.at[h, 1 - core], w_core.at[h], wc_s.at[d], wc_r.at[d], slab, partner)
            copy.start()
            near.append((d, h, copy))
        for d, h, copy in near:
            copy.wait_recv()
            if d > 0:
                total = grads[h, core].astype(f32) + w_core[h].astype(f32)
                w_to[d - 1] = total.astype(bf16)
                cross = remote(
                    w_to.at[d - 1], w_far.at[d - 1], wf_s.at[d - 1], wf_r.at[d - 1], slab, h * 2 + core
                )
                cross.start()
                w_cross.append(cross)
            sent.append(copy)

    sent += gather_rep(own, gathered, halves, pieces, gat_s, gat_r, halves_of_weights)
    def pick(g, h, j):
        dest = slot_block[slab_at(MID - g), g * SLOT_CAP + (h + core * halves) * per_rep + j]
        return gathered[lax.div(dest, own_blocks), lax.rem(dest, own_blocks)]

    second = {}
    for g in ORDER:
        for j in range(crossing):
            if g == MID:
                arrived[g, core, half, j] = pick(g, half, j)
            else:
                outgoing[g, j] = pick(g, half, j)
        if g != MID:
            second[g] = remote(
                outgoing.at[g],
                arrived.at[g, core, half, pl.ds(0, crossing)],
                slab_s.at[g],
                slab_r.at[g],
                slab_at(MID - g),
                rep,
            )
            second[g].start()
    direct = {}
    for g in ORDER:
        for h in range(halves):
            for j in range(crossing, per_rep):
                if g == MID:
                    arrived[g, core, h, j] = pick(g, h, j)
                else:
                    plain[g, h, j - crossing] = pick(g, h, j)
            if g != MID and crossing < per_rep:
                direct[g, h] = remote(
                    plain.at[g, h],
                    arrived.at[g, core, h, pl.ds(crossing, per_rep - crossing)],
                    plain_s.at[h, g],
                    plain_r.at[h, g],
                    slab_at(MID - g),
                    rep,
                )
                direct[g, h].start()
    total = grads[half, core].astype(f32) + w_core[half].astype(f32)
    for d, copy in enumerate(w_cross):
        copy.wait_recv()
        total = total + w_far[d].astype(f32)
    w_rep[...] = total.astype(bf16)
    w_slab = []
    for d in peers:
        peer = slab_at(d)
        copy = remote(w_rep.at[peer], w_in.at[d - 1], ws_s.at[d - 1], ws_r.at[d - 1], peer, rep)
        copy.start()
        w_slab.append(copy)
    w_back = []

    def finish_weights():
        total = w_rep[slab].astype(f32)
        for d, copy in enumerate(w_slab):
            copy.wait_recv()
            total = total + w_in[d].astype(f32)
        w_piece[...] = total.astype(bf16)
        summed[slab] = total.astype(bf16)
        for d in peers:
            copy = remote(
                w_piece, summed.at[slab], wg_s.at[d - 1], wg_r.at[d - 1], slab_at(d), rep
            )
            copy.start()
            w_back.append(copy)

    share(
        arrived,
        second,
        direct,
        crossing,
        far_s,
        far_r,
        on_s,
        on_r,
        straight_s,
        straight_r,
        halves,
        finish_weights,
    )
    for copy in w_back:
        copy.wait_recv()
    for copy in sent + w_cross + w_slab + w_back:
        copy.wait_send()


def fold_kernel(
    halves, part, summed, out, grads, from_core, outgoing, from_far, core_s, core_r, far_s, far_r, gat_s, gat_r
):
    slab, rep, core, half, partner = place()
    f32 = jnp.float32
    greet(rep_targets(halves))
    near = []
    for d in list(range(1, halves)) + [0]:
        h = lax.rem(half + d, halves)
        copy = remote(part.at[h, 1 - core], from_core.at[h], core_s.at[d], core_r.at[d], slab, partner)
        copy.start()
        near.append((d, h, copy))
    far = []

    def fold():
        for d, h, copy in near:
            copy.wait_recv()
            total = part[h, core].astype(f32) + from_core[h].astype(f32)
            if d == 0:
                out[...] = total
            else:
                outgoing[d - 1] = total.astype(jnp.bfloat16)
                onward = remote(
                    outgoing.at[d - 1],
                    from_far.at[d - 1],
                    far_s.at[d - 1],
                    far_r.at[d - 1],
                    slab,
                    h * 2 + core,
                )
                onward.start()
                far.append(onward)

    sent = gather_rep(summed, grads, halves, 1, gat_s, gat_r, fold)
    for d, onward in enumerate(far):
        onward.wait_recv()
        out[...] += from_far[d].astype(f32)
    for copy in sent + far + [copy for _, _, copy in near]:
        copy.wait_send()


def final_kernel(scale, base, folded, grads, grad_feats, g_gain, g_in, g_b, g_out):
    grad_feats[...] = base[...] + folded[...]
    width = grads.shape[1]

    def part(at, n):
        return grads[at : at + n].astype(jnp.float32) * scale

    n, panels = g_in.shape[0], g_in.shape[1] // width
    for c in range(panels):
        g_in[:, width * c : width * (c + 1)] = part(n * c, n)
    n = n * panels
    g_out[...] = part(n, g_out.shape[0])
    rest = part(n + g_out.shape[0], 16)
    at = 0
    for ref in (g_gain, g_b):
        for c in range(ref.shape[1] // width):
            ref[:, width * c : width * (c + 1)] = rest[at : at + 1]
            at += 1


def comm(kernel, cid, out_shape, in_specs, scratch):
    return pl.pallas_call(
        kernel,
        out_shape=out_shape,
        in_specs=in_specs,
        out_specs=jax.tree.map(lambda _: VMEM, out_shape),
        scratch_shapes=scratch,
        compiler_params=pltpu.CompilerParams(collective_id=cid, has_side_effects=True),
    )


def body(
    feats,
    cotangent,
    tile_table,
    edge_src,
    edge_tile,
    edge_slot,
    edge_count,
    slot_block,
    norm_gain,
    w_in,
    b_in,
    w_out,
):
    n_slab = lax.axis_size("slab")
    n_rep = lax.axis_size("rep")
    halves = n_rep // 2
    rows_dev, width = feats.shape
    hidden = w_out.shape[0]
    block_rows = tile_table.shape[1]
    own_blocks = rows_dev // block_rows
    slab_blocks = own_blocks * n_rep
    slot_count = slot_block.shape[1]
    per_rep = SLOT_CAP // n_rep
    pieces = 4
    bf16, f32 = jnp.bfloat16, jnp.float32
    lists = (edge_count, edge_src, edge_tile, edge_slot)
    shape = jax.ShapeDtypeStruct

    def block(*lead):
        return pltpu.VMEM((*lead, block_rows, width), bf16)

    n_gat = gather_sems(halves, pieces)
    slab_feats, turned = comm(
        functools.partial(gather_kernel, halves, pieces),
        0,
        (
            shape((n_rep, own_blocks, block_rows, width), bf16),
            shape(tile_table.shape, bf16),
        ),
        [VMEM, pl.BlockSpec(memory_space=pl.ANY)],
        [pltpu.VMEM(tile_table.shape, bf16), DMA] + [DMA((n_gat,))] * 2,
    )(feats.reshape(own_blocks, block_rows, width), tile_table)
    slab_feats = slab_feats.reshape(slab_blocks, block_rows, width)
    partial_sums = edges(False, slot_count, *lists, tile_table, slab_feats)
    arrived_shape = (NEIGH, 2, halves, per_rep, block_rows, width)
    share_sems = [DMA((halves - 1, NEIGH))] * 2 + [DMA((halves, NEIGH))] * 2
    arrived = comm(
        functools.partial(spread_kernel, halves),
        1,
        shape(arrived_shape, bf16),
        [VMEM],
        [
            block(NEIGH, halves, per_rep),
            block(halves - 1, NEIGH, per_rep),
            block(halves - 1, NEIGH, per_rep),
            block(NEIGH, per_rep),
        ]
        + [DMA((NEIGH,))] * 2
        + [DMA((halves - 1, NEIGH))] * 2
        + [DMA((NEIGH,))] * 2
        + share_sems,
    )(partial_sums.reshape(arrived_shape))
    used = w_in.size // width + hidden + 16
    each = -(-used // (n_slab * n_rep * 16)) * 16
    updated, base, d_agg, packed = pl.pallas_call(
        node_kernel,
        out_shape=(
            shape((rows_dev, width), bf16),
            shape((rows_dev, width), f32),
            shape((rows_dev, width), bf16),
            shape((n_slab * n_rep * each, width), bf16),
        ),
        in_specs=[SMEM] + [VMEM] * 7,
        out_specs=(VMEM,) * 4,
        scratch_shapes=[
            pltpu.VMEM((own_blocks, block_rows, width), f32),
            pltpu.VMEM(w_in.shape, f32),
            pltpu.VMEM(w_out.shape, f32),
            pltpu.VMEM((1, 2 * width), f32),
            pltpu.VMEM((1, hidden), f32),
        ],
    )(
        slot_block,
        arrived.reshape(slot_count, block_rows, width),
        feats,
        cotangent,
        norm_gain.reshape(1, -1),
        w_in,
        b_in.reshape(1, -1),
        w_out,
    )
    weights = pltpu.VMEM((n_slab, each, width), bf16)
    many = pltpu.VMEM((halves - 1, n_slab, each, width), bf16)
    slot_grads, summed = comm(
        functools.partial(return_kernel, halves, pieces),
        2,
        (shape(arrived_shape, bf16), shape((n_slab, each, width), bf16)),
        [SMEM, VMEM, VMEM],
        [
            block(n_rep, own_blocks),
            block(NEIGH, per_rep - per_rep // 2),
            block(NEIGH, halves, max(per_rep // 2, 1)),
            pltpu.VMEM((halves, n_slab, each, width), bf16),
            many,
            many,
            weights,
            pltpu.VMEM((n_slab - 1, each, width), bf16),
            pltpu.VMEM((each, width), bf16),
        ]
        + [DMA((n_gat,))] * 2
        + [DMA((NEIGH,))] * 2
        + share_sems
        + [DMA((halves, NEIGH))] * 4
        + [DMA((halves,))] * 2
        + [DMA((halves - 1,))] * 2
        + [DMA((n_slab - 1,))] * 4,
    )(
        slot_block,
        d_agg.reshape(own_blocks, block_rows, width),
        packed.reshape(halves, 2, n_slab, each, width),
    )
    from_edges = edges(
        True, slab_blocks, *lists, turned, slot_grads.reshape(slot_count, block_rows, width)
    )
    n_sum = gather_sems(halves, 1)
    folded, grads = comm(
        functools.partial(fold_kernel, halves),
        3,
        (shape((rows_dev, width), f32), shape((n_rep, n_slab, each, width), bf16)),
        [VMEM, VMEM],
        [
            pltpu.VMEM((halves, rows_dev, width), bf16),
            pltpu.VMEM((halves - 1, rows_dev, width), bf16),
            pltpu.VMEM((halves - 1, rows_dev, width), bf16),
        ]
        + [DMA((halves,))] * 2
        + [DMA((halves - 1,))] * 2
        + [DMA((n_sum,))] * 2,
    )(from_edges.reshape(halves, 2, rows_dev, width), summed)
    scale = float(rows_dev * n_slab * n_rep) ** (-0.5)
    grad_feats, grad_gain, grad_w_in, grad_b_in, grad_w_out = pl.pallas_call(
        functools.partial(final_kernel, scale),
        out_shape=(
            shape((rows_dev, width), f32),
            shape((1, 2 * width), f32),
            shape(w_in.shape, f32),
            shape((1, hidden), f32),
            shape(w_out.shape, f32),
        ),
        in_specs=[VMEM] * 3,
        out_specs=(VMEM,) * 5,
    )(base, folded, grads.reshape(-1, width))
    return (
        updated,
        grad_feats,
        grad_gain.reshape(-1),
        grad_w_in,
        grad_b_in.reshape(-1),
        grad_w_out,
    )


def solution(mesh):
    placed = (
        P(("slab", "rep"), None),
        P(("slab", "rep"), None),
        P(("slab", "rep"), None, None),
        P(("slab", "rep"), None),
        P(("slab", "rep"), None),
        P(("slab", "rep"), None),
        P(("slab", "rep")),
        P(),
        P(),
        P(),
        P(),
        P(),
    )
    return jax.shard_map(
        body,
        mesh=mesh,
        in_specs=placed,
        out_specs=(P(("slab", "rep"), None), P(("slab", "rep"), None), P(), P(), P(), P()),
        check_vma=False,
    )
```

```python
import functools

import jax
import jax.numpy as jnp
from jax import lax
from jax.experimental import pallas as pl
from jax.experimental.pallas import tpu as pltpu
from jax.sharding import PartitionSpec as P

NEIGH = 8
SLOT_CAP = 8
MID = NEIGH // 2

RMS_EPS = 1e-06
EDGE_UNROLL = 8
AXES = ("slab", "rep")
VMEM = pl.BlockSpec(memory_space=pltpu.VMEM)
SMEM = pl.BlockSpec(memory_space=pltpu.SMEM)
DMA = pltpu.SemaphoreType.DMA


def remote(src, dst, send_sem, recv_sem, slab, rep):
    return pltpu.make_async_remote_copy(
        src_ref=src,
        dst_ref=dst,
        send_sem=send_sem,
        recv_sem=recv_sem,
        device_id=(slab, rep),
        device_id_type=pl.DeviceIdType.MESH,
    )


def greet(targets):
    barrier = pltpu.get_barrier_semaphore()
    for slab, rep in targets:
        pl.semaphore_signal(
            barrier, inc=1, device_id=(slab, rep), device_id_type=pl.DeviceIdType.MESH
        )
    pl.semaphore_wait(barrier, len(targets))


def place():
    slab, rep = lax.axis_index("slab"), lax.axis_index("rep")
    core = lax.rem(rep, 2)
    return slab, rep, core, lax.div(rep, 2), rep + 1 - 2 * core


def gather_rep(own, out, halves, pieces, send_sems, recv_sems, meanwhile):
    slab, rep, core, half, partner = place()
    rows = own.shape[0] // pieces

    def piece(ref, i):
        return ref.at[pl.ds(i * rows, rows)]

    far = []
    sems = 0
    for d in range(1, halves):
        peer = lax.rem(half + d, halves) * 2 + core
        for i in range(pieces):
            copy = remote(
                piece(own, i), piece(out.at[rep], i), send_sems.at[sems], recv_sems.at[sems], slab, peer
            )
            copy.start()
            far.append((copy, lax.rem(half + halves - d, halves) * 2 + core, i))
            sems += 1
    near = remote(own, out.at[rep], send_sems.at[sems], recv_sems.at[sems], slab, partner)
    near.start()
    sems += 1
    out[rep] = own[...]
    meanwhile()
    passed = [near]
    for copy, origin, i in far:
        copy.wait_recv()
        onward = remote(
            piece(out.at[origin], i),
            piece(out.at[origin], i),
            send_sems.at[sems],
            recv_sems.at[sems],
            slab,
            partner,
        )
        onward.start()
        passed.append(onward)
        sems += 1
    for copy in passed:
        copy.wait_recv()
    return [copy for copy, _, _ in far] + passed


def gather_sems(halves, pieces):
    return 2 * (halves - 1) * pieces + 1


def rep_targets(halves):
    slab, rep, core, half, partner = place()
    return [(slab, partner)] + [
        (slab, lax.rem(half + d, halves) * 2 + core) for d in range(1, halves)
    ]


def gather_kernel(halves, pieces, own, table_hbm, out, turned, table, table_sem, send_sems, recv_sems):
    load = pltpu.make_async_copy(table_hbm, table, table_sem)
    load.start()
    greet(rep_targets(halves))

    def meanwhile():
        load.wait()

        @pl.loop(0, table.shape[0])
        def _(t):
            turned[t] = table[t].T

    for copy in gather_rep(own, out, halves, pieces, send_sems, recv_sems, meanwhile):
        copy.wait_send()


def edge_kernel(by_slot, n_out, count, srcs, tiles, slots, table, given, out, acc):
    live = count[0]
    last = srcs.shape[1] - 1
    acc[...] = jnp.zeros_like(acc)

    def turn(i, carry):
        work = []
        for u in range(EDGE_UNROLL):
            at = i * EDGE_UNROLL + u
            e = jnp.minimum(at, last)
            src, slot = srcs[0, e], slots[0, e]
            read, write = (slot, src) if by_slot else (src, slot)
            product = jnp.dot(table[tiles[0, e]], given[read], preferred_element_type=jnp.float32)
            work.append((jnp.where(at < live, write, n_out), product))
        for write, product in work:
            acc[write] += product
        return carry

    lax.fori_loop(0, lax.div(live + EDGE_UNROLL - 1, EDGE_UNROLL), turn, 0)
    out[...] = acc[0:n_out].astype(out.dtype)


def edges(by_slot, n_out, count, srcs, tiles, slots, table, given):
    shape = (table.shape[1], given.shape[2])
    return pl.pallas_call(
        functools.partial(edge_kernel, by_slot, n_out),
        out_shape=jax.ShapeDtypeStruct((n_out, *shape), jnp.bfloat16),
        in_specs=[SMEM] * 4 + [VMEM] * 2,
        out_specs=VMEM,
        scratch_shapes=[pltpu.VMEM((n_out + 1, *shape), jnp.float32)],
    )(count, srcs, tiles, slots, table, given)


def slab_at(offset):
    n_slab = lax.axis_size("slab")
    return lax.rem(lax.axis_index("slab") + offset + n_slab, n_slab)


FAR_FIRST = sorted((g for g in range(NEIGH) if g != MID), key=lambda g: -abs(g - MID))
ORDER = FAR_FIRST + [MID]


def share(arrived, second, direct, crossing, far_s, far_r, on_s, on_r, straight_s, straight_r, halves, meanwhile):
    slab, rep, core, half, partner = place()
    order = [MID] + FAR_FIRST
    copies = []
    across = []
    for g in order:
        if g in second:
            second[g].wait_recv()
        own = arrived.at[g, core, half, pl.ds(0, crossing)]
        for d in range(1, halves):
            peer = lax.rem(half + d, halves) * 2 + core
            copy = remote(own, own, far_s.at[d - 1, g], far_r.at[d - 1, g], slab, peer)
            copy.start()
            across.append((g, d, copy))
        copy = remote(own, own, on_s.at[0, g], on_r.at[0, g], slab, partner)
        copy.start()
        copies.append(copy)
    meanwhile()
    for g, d, copy in across:
        copy.wait_recv()
        theirs = arrived.at[g, core, lax.rem(half + halves - d, halves), pl.ds(0, crossing)]
        onward = remote(theirs, theirs, on_s.at[d, g], on_r.at[d, g], slab, partner)
        onward.start()
        copies.append(onward)
    others = arrived.shape[3] - crossing
    if others:
        for g in order:
            for h in range(halves):
                if (g, h) in direct:
                    direct[g, h].wait_recv()
                here = arrived.at[g, core, h, pl.ds(crossing, others)]
                onward = remote(here, here, straight_s.at[h, g], straight_r.at[h, g], slab, partner)
                onward.start()
                copies.append(onward)
    for copy in copies:
        copy.wait_recv()
    sent = copies + [copy for _, _, copy in across] + list(second.values()) + list(direct.values())
    for copy in sent:
        copy.wait_send()


def spread_kernel(
    halves,
    part,
    arrived,
    from_core,
    to_far,
    from_far,
    outgoing,
    core_s,
    core_r,
    fold_s,
    fold_r,
    slab_s,
    slab_r,
    far_s,
    far_r,
    on_s,
    on_r,
):
    slab, rep, core, half, partner = place()
    greet(rep_targets(halves) + [(slab_at(MID - g), rep) for g in FAR_FIRST])
    f32 = jnp.float32
    first = {}
    for g in ORDER:
        first[g] = remote(
            part.at[g, 1 - core], from_core.at[g], core_s.at[g], core_r.at[g], slab, partner
        )
        first[g].start()
    cross = {}
    for g in ORDER:
        first[g].wait_recv()
        for d in range(1, halves):
            h = lax.rem(half + d, halves)
            total = part[g, core, h].astype(f32) + from_core[g, h].astype(f32)
            to_far[d - 1, g] = total.astype(jnp.bfloat16)
            cross[g, d] = remote(
                to_far.at[d - 1, g],
                from_far.at[d - 1, g],
                fold_s.at[d - 1, g],
                fold_r.at[d - 1, g],
                slab,
                h * 2 + core,
            )
            cross[g, d].start()
    second = {}
    for g in ORDER:
        total = part[g, core, half].astype(f32) + from_core[g, half].astype(f32)
        for d in range(1, halves):
            cross[g, d].wait_recv()
            total = total + from_far[d - 1, g].astype(f32)
        if g == MID:
            arrived[g, core, half] = total.astype(jnp.bfloat16)
        else:
            outgoing[g] = total.astype(jnp.bfloat16)
            second[g] = remote(
                outgoing.at[g],
                arrived.at[g, core, half],
                slab_s.at[g],
                slab_r.at[g],
                slab_at(g - MID),
                rep,
            )
            second[g].start()
    share(
        arrived,
        second,
        {},
        arrived.shape[3],
        far_s,
        far_r,
        on_s,
        on_r,
        None,
        None,
        halves,
        lambda: None,
    )
    for copy in list(first.values()) + list(cross.values()):
        copy.wait_send()


def node_kernel(
    slot_block,
    arrived,
    feats,
    cot,
    gain,
    w_in,
    b_in,
    w_out,
    updated,
    base,
    d_agg,
    packed,
    agg,
    g_in,
    g_out,
    g_gain,
    g_b,
):
    slab, rep = lax.axis_index("slab"), lax.axis_index("rep")
    f32, bf16 = jnp.float32, jnp.bfloat16
    own_blocks, block_rows, width = agg.shape
    n_slab = slot_block.shape[0]
    agg[...] = jnp.zeros_like(agg)

    @pl.loop(0, NEIGH * SLOT_CAP)
    def _(c):
        origin = lax.rem(slab - (lax.div(c, SLOT_CAP) - MID) + n_slab, n_slab)
        dest = slot_block[origin, c]

        @pl.when(lax.div(dest, own_blocks) == rep)
        def _():
            agg[lax.rem(dest, own_blocks)] += arrived[c].astype(f32)

    for ref in (g_in, g_out, g_gain, g_b):
        ref[...] = jnp.zeros_like(ref)
    step_blocks = 2 if own_blocks % 2 == 0 else 1
    rows = step_blocks * block_rows

    @pl.loop(0, own_blocks // step_blocks)
    def _(i):
        at = pl.ds(pl.multiple_of(i * rows, rows), rows)
        feat = feats[at].astype(f32)
        cots = cot[at]
        wide = jnp.concatenate(
            [feat, agg[pl.ds(i * step_blocks, step_blocks)].reshape(rows, width)], axis=1
        )
        inv = lax.rsqrt(jnp.mean(wide * wide, axis=1, keepdims=True) + RMS_EPS)
        scaled = wide * inv
        normed = (scaled * gain[...]).astype(bf16)
        pre = jnp.dot(normed, w_in[...], preferred_element_type=f32) + b_in[...]
        sg = jax.nn.sigmoid(pre)
        act = (pre * sg).astype(bf16)
        updated[at] = (feat + jnp.dot(act, w_out[...], preferred_element_type=f32)).astype(bf16)
        d_act = lax.dot_general(cots, w_out[...], (((1,), (1,)), ((), ())), preferred_element_type=f32)
        d_pre = d_act * sg * (1.0 + pre * (1.0 - sg))
        d_pre_b = d_pre.astype(bf16)
        d_normed = lax.dot_general(
            d_pre_b, w_in[...], (((1,), (1,)), ((), ())), preferred_element_type=f32
        )
        d_scaled = d_normed * gain[...]
        inner = jnp.mean(d_scaled * wide, axis=1, keepdims=True)
        d_wide = inv * d_scaled - inv * inv * inv * wide * inner
        base[at] = cots.astype(f32) + d_wide[:, :width]
        d_agg[at] = d_wide[:, width:].astype(bf16)
        g_in[...] += lax.dot_general(normed, d_pre_b, (((0,), (0,)), ((), ())), preferred_element_type=f32)
        g_out[...] += lax.dot_general(act, cots, (((0,), (0,)), ((), ())), preferred_element_type=f32)
        g_gain[...] += jnp.sum(d_normed * scaled, axis=0, keepdims=True)
        g_b[...] += jnp.sum(d_pre, axis=0, keepdims=True)

    packed[...] = jnp.zeros_like(packed)
    n = g_in.shape[0]
    for c in range(g_in.shape[1] // width):
        packed[n * c : n * (c + 1)] = g_in[:, width * c : width * (c + 1)].astype(bf16)
    n = n * (g_in.shape[1] // width)
    packed[n : n + g_out.shape[0]] = g_out[...].astype(bf16)
    n += g_out.shape[0]
    rest = [
        ref[:, width * c : width * (c + 1)]
        for ref in (g_gain, g_b)
        for c in range(ref.shape[1] // width)
    ]
    rest.append(jnp.zeros((16 - len(rest), width), f32))
    packed[n : n + 16] = jnp.concatenate(rest, axis=0).astype(bf16)


def return_kernel(
    halves,
    pieces,
    slot_block,
    own,
    grads,
    arrived,
    summed,
    gathered,
    outgoing,
    plain,
    w_core,
    w_to,
    w_far,
    w_rep,
    w_in,
    w_piece,
    gat_s,
    gat_r,
    slab_s,
    slab_r,
    far_s,
    far_r,
    on_s,
    on_r,
    plain_s,
    plain_r,
    straight_s,
    straight_r,
    wc_s,
    wc_r,
    wf_s,
    wf_r,
    ws_s,
    ws_r,
    wg_s,
    wg_r,
):
    slab, rep, core, half, partner = place()
    n_slab = slot_block.shape[0]
    peers = range(1, n_slab)
    greet(rep_targets(halves) + [(slab_at(d), rep) for d in peers])
    f32, bf16 = jnp.float32, jnp.bfloat16
    own_blocks = own.shape[0]
    per_rep = arrived.shape[3]
    crossing = outgoing.shape[1]
    sent = []
    w_cross = []

    def halves_of_weights():
        near = []
        for d in list(range(1, halves)) + [0]:
            h = lax.rem(half + d, halves)
            copy = remote(grads.at[h, 1 - core], w_core.at[h], wc_s.at[d], wc_r.at[d], slab, partner)
            copy.start()
            near.append((d, h, copy))
        for d, h, copy in near:
            copy.wait_recv()
            if d > 0:
                total = grads[h, core].astype(f32) + w_core[h].astype(f32)
                w_to[d - 1] = total.astype(bf16)
                cross = remote(
                    w_to.at[d - 1], w_far.at[d - 1], wf_s.at[d - 1], wf_r.at[d - 1], slab, h * 2 + core
                )
                cross.start()
                w_cross.append(cross)
            sent.append(copy)

    sent += gather_rep(own, gathered, halves, pieces, gat_s, gat_r, halves_of_weights)
    def pick(g, h, j):
        dest = slot_block[slab_at(MID - g), g * SLOT_CAP + (h + core * halves) * per_rep + j]
        return gathered[lax.div(dest, own_blocks), lax.rem(dest, own_blocks)]

    second = {}
    for g in ORDER:
        for j in range(crossing):
            if g == MID:
                arrived[g, core, half, j] = pick(g, half, j)
            else:
                outgoing[g, j] = pick(g, half, j)
        if g != MID:
            second[g] = remote(
                outgoing.at[g],
                arrived.at[g, core, half, pl.ds(0, crossing)],
                slab_s.at[g],
                slab_r.at[g],
                slab_at(MID - g),
                rep,
            )
            second[g].start()
    direct = {}
    for g in ORDER:
        for h in range(halves):
            for j in range(crossing, per_rep):
                if g == MID:
                    arrived[g, core, h, j] = pick(g, h, j)
                else:
                    plain[g, h, j - crossing] = pick(g, h, j)
            if g != MID and crossing < per_rep:
                direct[g, h] = remote(
                    plain.at[g, h],
                    arrived.at[g, core, h, pl.ds(crossing, per_rep - crossing)],
                    plain_s.at[h, g],
                    plain_r.at[h, g],
                    slab_at(MID - g),
                    rep,
                )
                direct[g, h].start()
    total = grads[half, core].astype(f32) + w_core[half].astype(f32)
    for d, copy in enumerate(w_cross):
        copy.wait_recv()
        total = total + w_far[d].astype(f32)
    w_rep[...] = total.astype(bf16)
    w_slab = []
    for d in peers:
        peer = slab_at(d)
        copy = remote(w_rep.at[peer], w_in.at[d - 1], ws_s.at[d - 1], ws_r.at[d - 1], peer, rep)
        copy.start()
        w_slab.append(copy)
    w_back = []

    def finish_weights():
        total = w_rep[slab].astype(f32)
        for d, copy in enumerate(w_slab):
            copy.wait_recv()
            total = total + w_in[d].astype(f32)
        w_piece[...] = total.astype(bf16)
        summed[slab] = total.astype(bf16)
        for d in peers:
            copy = remote(
                w_piece, summed.at[slab], wg_s.at[d - 1], wg_r.at[d - 1], slab_at(d), rep
            )
            copy.start()
            w_back.append(copy)

    share(
        arrived,
        second,
        direct,
        crossing,
        far_s,
        far_r,
        on_s,
        on_r,
        straight_s,
        straight_r,
        halves,
        finish_weights,
    )
    for copy in w_back:
        copy.wait_recv()
    for copy in sent + w_cross + w_slab + w_back:
        copy.wait_send()


def fold_kernel(
    halves, part, summed, out, grads, from_core, outgoing, from_far, core_s, core_r, far_s, far_r, gat_s, gat_r
):
    slab, rep, core, half, partner = place()
    f32 = jnp.float32
    greet(rep_targets(halves))
    near = []
    for d in list(range(1, halves)) + [0]:
        h = lax.rem(half + d, halves)
        copy = remote(part.at[h, 1 - core], from_core.at[h], core_s.at[d], core_r.at[d], slab, partner)
        copy.start()
        near.append((d, h, copy))
    far = []

    def fold():
        for d, h, copy in near:
            copy.wait_recv()
            total = part[h, core].astype(f32) + from_core[h].astype(f32)
            if d == 0:
                out[...] = total
            else:
                outgoing[d - 1] = total.astype(jnp.bfloat16)
                onward = remote(
                    outgoing.at[d - 1],
                    from_far.at[d - 1],
                    far_s.at[d - 1],
                    far_r.at[d - 1],
                    slab,
                    h * 2 + core,
                )
                onward.start()
                far.append(onward)

    sent = gather_rep(summed, grads, halves, 1, gat_s, gat_r, fold)
    for d, onward in enumerate(far):
        onward.wait_recv()
        out[...] += from_far[d].astype(f32)
    for copy in sent + far + [copy for _, _, copy in near]:
        copy.wait_send()


def final_kernel(scale, base, folded, grads, grad_feats, g_gain, g_in, g_b, g_out):
    grad_feats[...] = base[...] + folded[...]
    width = grads.shape[1]

    def part(at, n):
        return grads[at : at + n].astype(jnp.float32) * scale

    n, panels = g_in.shape[0], g_in.shape[1] // width
    for c in range(panels):
        g_in[:, width * c : width * (c + 1)] = part(n * c, n)
    n = n * panels
    g_out[...] = part(n, g_out.shape[0])
    rest = part(n + g_out.shape[0], 16)
    at = 0
    for ref in (g_gain, g_b):
        for c in range(ref.shape[1] // width):
            ref[:, width * c : width * (c + 1)] = rest[at : at + 1]
            at += 1


def comm(kernel, cid, out_shape, in_specs, scratch):
    return pl.pallas_call(
        kernel,
        out_shape=out_shape,
        in_specs=in_specs,
        out_specs=jax.tree.map(lambda _: VMEM, out_shape),
        scratch_shapes=scratch,
        compiler_params=pltpu.CompilerParams(collective_id=cid, has_side_effects=True),
    )


def body(
    feats,
    cotangent,
    tile_table,
    edge_src,
    edge_tile,
    edge_slot,
    edge_count,
    slot_block,
    norm_gain,
    w_in,
    b_in,
    w_out,
):
    n_slab = lax.axis_size("slab")
    n_rep = lax.axis_size("rep")
    halves = n_rep // 2
    rows_dev, width = feats.shape
    hidden = w_out.shape[0]
    block_rows = tile_table.shape[1]
    own_blocks = rows_dev // block_rows
    slab_blocks = own_blocks * n_rep
    slot_count = slot_block.shape[1]
    per_rep = SLOT_CAP // n_rep
    pieces = 4
    bf16, f32 = jnp.bfloat16, jnp.float32
    lists = (edge_count, edge_src, edge_tile, edge_slot)
    shape = jax.ShapeDtypeStruct

    def block(*lead):
        return pltpu.VMEM((*lead, block_rows, width), bf16)

    n_gat = gather_sems(halves, pieces)
    slab_feats, turned = comm(
        functools.partial(gather_kernel, halves, pieces),
        0,
        (
            shape((n_rep, own_blocks, block_rows, width), bf16),
            shape(tile_table.shape, bf16),
        ),
        [VMEM, pl.BlockSpec(memory_space=pl.ANY)],
        [pltpu.VMEM(tile_table.shape, bf16), DMA] + [DMA((n_gat,))] * 2,
    )(feats.reshape(own_blocks, block_rows, width), tile_table)
    slab_feats = slab_feats.reshape(slab_blocks, block_rows, width)
    partial_sums = edges(False, slot_count, *lists, tile_table, slab_feats)
    arrived_shape = (NEIGH, 2, halves, per_rep, block_rows, width)
    share_sems = [DMA((halves - 1, NEIGH))] * 2 + [DMA((halves, NEIGH))] * 2
    arrived = comm(
        functools.partial(spread_kernel, halves),
        1,
        shape(arrived_shape, bf16),
        [VMEM],
        [
            block(NEIGH, halves, per_rep),
            block(halves - 1, NEIGH, per_rep),
            block(halves - 1, NEIGH, per_rep),
            block(NEIGH, per_rep),
        ]
        + [DMA((NEIGH,))] * 2
        + [DMA((halves - 1, NEIGH))] * 2
        + [DMA((NEIGH,))] * 2
        + share_sems,
    )(partial_sums.reshape(arrived_shape))
    used = w_in.size // width + hidden + 16
    each = -(-used // (n_slab * n_rep * 16)) * 16
    updated, base, d_agg, packed = pl.pallas_call(
        node_kernel,
        out_shape=(
            shape((rows_dev, width), bf16),
            shape((rows_dev, width), f32),
            shape((rows_dev, width), bf16),
            shape((n_slab * n_rep * each, width), bf16),
        ),
        in_specs=[SMEM] + [VMEM] * 7,
        out_specs=(VMEM,) * 4,
        scratch_shapes=[
            pltpu.VMEM((own_blocks, block_rows, width), f32),
            pltpu.VMEM(w_in.shape, f32),
            pltpu.VMEM(w_out.shape, f32),
            pltpu.VMEM((1, 2 * width), f32),
            pltpu.VMEM((1, hidden), f32),
        ],
    )(
        slot_block,
        arrived.reshape(slot_count, block_rows, width),
        feats,
        cotangent,
        norm_gain.reshape(1, -1),
        w_in,
        b_in.reshape(1, -1),
        w_out,
    )
    weights = pltpu.VMEM((n_slab, each, width), bf16)
    many = pltpu.VMEM((halves - 1, n_slab, each, width), bf16)
    slot_grads, summed = comm(
        functools.partial(return_kernel, halves, pieces),
        2,
        (shape(arrived_shape, bf16), shape((n_slab, each, width), bf16)),
        [SMEM, VMEM, VMEM],
        [
            block(n_rep, own_blocks),
            block(NEIGH, per_rep),
            block(NEIGH, halves, max(per_rep // 2, 1)),
            pltpu.VMEM((halves, n_slab, each, width), bf16),
            many,
            many,
            weights,
            pltpu.VMEM((n_slab - 1, each, width), bf16),
            pltpu.VMEM((each, width), bf16),
        ]
        + [DMA((n_gat,))] * 2
        + [DMA((NEIGH,))] * 2
        + share_sems
        + [DMA((halves, NEIGH))] * 4
        + [DMA((halves,))] * 2
        + [DMA((halves - 1,))] * 2
        + [DMA((n_slab - 1,))] * 4,
    )(
        slot_block,
        d_agg.reshape(own_blocks, block_rows, width),
        packed.reshape(halves, 2, n_slab, each, width),
    )
    from_edges = edges(
        True, slab_blocks, *lists, turned, slot_grads.reshape(slot_count, block_rows, width)
    )
    n_sum = gather_sems(halves, 1)
    folded, grads = comm(
        functools.partial(fold_kernel, halves),
        3,
        (shape((rows_dev, width), f32), shape((n_rep, n_slab, each, width), bf16)),
        [VMEM, VMEM],
        [
            pltpu.VMEM((halves, rows_dev, width), bf16),
            pltpu.VMEM((halves - 1, rows_dev, width), bf16),
            pltpu.VMEM((halves - 1, rows_dev, width), bf16),
        ]
        + [DMA((halves,))] * 2
        + [DMA((halves - 1,))] * 2
        + [DMA((n_sum,))] * 2,
    )(from_edges.reshape(halves, 2, rows_dev, width), summed)
    scale = float(rows_dev * n_slab * n_rep) ** (-0.5)
    grad_feats, grad_gain, grad_w_in, grad_b_in, grad_w_out = pl.pallas_call(
        functools.partial(final_kernel, scale),
        out_shape=(
            shape((rows_dev, width), f32),
            shape((1, 2 * width), f32),
            shape(w_in.shape, f32),
            shape((1, hidden), f32),
            shape(w_out.shape, f32),
        ),
        in_specs=[VMEM] * 3,
        out_specs=(VMEM,) * 5,
    )(base, folded, grads.reshape(-1, width))
    return (
        updated,
        grad_feats,
        grad_gain.reshape(-1),
        grad_w_in,
        grad_b_in.reshape(-1),
        grad_w_out,
    )


def solution(mesh):
    placed = (
        P(("slab", "rep"), None),
        P(("slab", "rep"), None),
        P(("slab", "rep"), None, None),
        P(("slab", "rep"), None),
        P(("slab", "rep"), None),
        P(("slab", "rep"), None),
        P(("slab", "rep")),
        P(),
        P(),
        P(),
        P(),
        P(),
    )
    return jax.shard_map(
        body,
        mesh=mesh,
        in_specs=placed,
        out_specs=(P(("slab", "rep"), None), P(("slab", "rep"), None), P(), P(), P(), P()),
        check_vma=False,
    )
```
